32 devices in a mesh: loop: 8 (over y, x, core), ctx: 4 (over z).
Axes of the slice: x: 2, y: 2, z: 4, core: 2. Of those that a mesh axis runs over, the one named last changes fastest.
Arguments:
- tokens: bfloat16 [4096, 3072], P(('loop', 'ctx')), may hold values from -6 to 6
- cotangent: bfloat16 [4096, 3072], P(('loop', 'ctx')), may hold values from -6 to 6
- gain: float32 [3072], replicated, may hold values from 0.1 to 1.9
- weights: bfloat16 [3072, 4, 3072], P('loop', None, 'ctx'), may hold values from -100 to 100
Outputs:
- d_tokens: bfloat16 [4096, 3072], P(('loop', 'ctx'))
- weight_grads: float32 [3072, 4, 3072], P('loop', None, 'ctx')
- gain_grad: float32 [3072], replicated
The draws below stay inside these ranges and needn't reach their ends.
All inputs are finite; a program needn't handle non-finite values.
Results may differ from the reference program's by a relative error of at most 0.015.
Values may be sent and summed in bfloat16 or wider, within the bound.
No kernel may reach another device: no remote copies, remote signals or barrier semaphores. Data moves between devices by JAX's collectives and lax.ppermute only.
A program may use at most 128 MiB of HBM per device.

```python
import math
import jax
import jax.numpy as jnp
from jax import lax

D = 3072
HEADS = 24
HD = 128
TOK_DEV = 128
TOKENS = 4096
N_LOOP = 8
N_CTX = 4


def draw_weights(key, part):
    base = jax.random.truncated_normal(key, -4.0, 4.0, (D, 4, HEADS * HD), jnp.float32) * D ** (-0.5)
    return base.astype(jnp.bfloat16)


def steps_of(own_key, extent, shards, low, top_value):
    level, own = 1.0, jax.random.fold_in(own_key, 6)
    for dim, parts in shards:
        draws = jnp.exp(jax.random.uniform(jax.random.fold_in(own, dim), (parts,), jnp.float32, low / len(shards), top_value / len(shards)))
        level = level * jnp.repeat(draws, extent[dim] // parts).reshape([-1 if axis == dim else 1 for axis in range(len(extent))])
    return level


def noise(stream_key, extent, scale, reach, shards=(), held_as=jnp.bfloat16):
    factor_of = steps_of(stream_key, extent, shards, -0.22, 0.18) if shards else 1.0
    entries = jax.random.normal(stream_key, extent, jnp.float32) * scale * factor_of
    return jnp.minimum(jnp.maximum(entries, -reach), reach).astype(held_as)


def setup_inputs(seed: int = 0) -> dict:
    seeds = jax.random.split(jax.random.key(seed), 5)
    return {
        "tokens": noise(seeds[0], (TOKENS, D), 1.0, 6.0, ((0, 32),)),
        "cotangent": noise(seeds[1], (TOKENS, D), 1.0, 6.0, ((0, 32),)),
        "gain": jnp.clip(1.0 + 0.18 * jax.random.normal(seeds[2], (D,), jnp.float32), 0.1, 1.9),
        "weights": draw_weights(jax.random.fold_in(seeds[4], 71), 0),
    }


EPS = 1e-05

def norm_rows(row_values, gain):
    values_f = row_values.astype(jnp.float32)
    inverse = lax.rsqrt(lax.optimization_barrier(jnp.mean(values_f * values_f, axis=1, keepdims=True)) + EPS)
    return (inverse, (values_f * inverse * gain).astype(jnp.bfloat16))

def rotate(values_f, offset, direction):
    amount = values_f.shape[0]
    half_width = values_f.shape[1] // 2
    position = (offset + jnp.arange(amount)).astype(jnp.float32)
    rates = jnp.exp(-math.log(10000.0) * jnp.arange(half_width).astype(jnp.float32) * 2.0 / values_f.shape[1])
    angle = position[:, None] * rates[None, :]
    cosine = jnp.cos(angle)
    sine = jnp.sin(angle) * direction
    first_half = values_f[:, :half_width]
    second_half = values_f[:, half_width:]
    return jnp.concatenate([first_half * cosine - second_half * sine, second_half * cosine + first_half * sine], axis=1)

def head_work(packed):
    query_head, key_head, value_head, grad_head = packed
    seq_rows = query_head.shape[0]
    width = query_head.shape[1]
    block_rows = min(512, seq_rows)
    scale = 1.0 / math.sqrt(width)
    rot_keys = rotate(key_head.astype(jnp.float32), 0, 1.0).astype(jnp.bfloat16)
    col_place = jnp.arange(seq_rows)

    def one_block(number):
        first_row = number * block_rows
        query_part = lax.dynamic_slice_in_dim(query_head, first_row, block_rows, 0).astype(jnp.float32)
        grad_part = lax.dynamic_slice_in_dim(grad_head, first_row, block_rows, 0)
        rot_query = rotate(query_part, first_row, 1.0).astype(jnp.bfloat16)
        scores = lax.dot_general(rot_query, rot_keys, (((1,), (1,)), ((), ())), preferred_element_type=jnp.float32) * scale
        row_place = first_row + jnp.arange(block_rows)
        scores = jnp.where(col_place[None, :] <= row_place[:, None], scores, -1e+30)
        maximum = lax.optimization_barrier(jnp.max(scores, axis=1, keepdims=True))
        expo = jnp.exp(scores - maximum)
        probs = expo / lax.optimization_barrier(jnp.sum(expo, axis=1, keepdims=True))
        probs_low = probs.astype(jnp.bfloat16)
        output = jnp.dot(probs_low, value_head, preferred_element_type=jnp.float32)
        d_probs = lax.dot_general(grad_part, value_head, (((1,), (1,)), ((), ())), preferred_element_type=jnp.float32)
        delta = lax.optimization_barrier(jnp.sum(grad_part.astype(jnp.float32) * output, axis=1, keepdims=True))
        d_scores = (probs * (d_probs - delta) * scale).astype(jnp.bfloat16)
        grad_query = rotate(jnp.dot(d_scores, rot_keys, preferred_element_type=jnp.float32), first_row, -1.0)
        rot_key_grad = lax.dot_general(d_scores, rot_query, (((0,), (0,)), ((), ())), preferred_element_type=jnp.float32)
        grad_values = lax.dot_general(probs_low, grad_part, (((0,), (0,)), ((), ())), preferred_element_type=jnp.float32)
        return (output, grad_query, rot_key_grad, grad_values)
    outputs, grad_query, rot_key_grad, grad_values = lax.map(one_block, jnp.arange(seq_rows // block_rows))
    grad_keys = rotate(lax.optimization_barrier(jnp.sum(rot_key_grad, axis=0)), 0, -1.0)
    return (outputs.reshape(seq_rows, width), grad_query.reshape(seq_rows, width), grad_keys, lax.optimization_barrier(jnp.sum(grad_values, axis=0)))

def sequence_grads(row_values, cot_rows, gain, weights):
    seq_rows = row_values.shape[0]
    inverse, normed = norm_rows(row_values, gain)
    projected = [jnp.dot(normed, weights[:, member, :], preferred_element_type=jnp.float32).astype(jnp.bfloat16) for member in range(3)]
    d_attn = jnp.dot(cot_rows, weights[:, 3, :], preferred_element_type=jnp.float32).astype(jnp.bfloat16)

    def split_heads(matrix):
        return matrix.reshape(seq_rows, HEADS, HD).transpose(1, 0, 2)

    def merge_heads(matrix):
        return matrix.transpose(1, 0, 2).reshape(seq_rows, HEADS * HD).astype(jnp.bfloat16)
    attn, grad_query, grad_keys, grad_values = lax.map(head_work, (split_heads(projected[0]), split_heads(projected[1]), split_heads(projected[2]), split_heads(d_attn)))
    attn = merge_heads(attn)
    grads = [merge_heads(grad_query), merge_heads(grad_keys), merge_heads(grad_values)]
    terms = [jnp.einsum('sd,sc->dc', normed, grads[member], preferred_element_type=jnp.float32) for member in range(3)]
    terms.append(jnp.einsum('sd,sc->dc', cot_rows, attn, preferred_element_type=jnp.float32))
    seq_terms = jnp.stack(terms, axis=1).astype(jnp.bfloat16)
    group_width = HEADS * HD // N_CTX
    d_normed = jnp.zeros((seq_rows, D), jnp.float32)
    for group in range(N_CTX):
        low = group * group_width
        partial_sum = jnp.zeros((seq_rows, D), jnp.float32)
        for member in range(3):
            partial_sum = partial_sum + lax.dot_general(grads[member][:, low:low + group_width], weights[:, member, low:low + group_width], (((1,), (1,)), ((), ())), preferred_element_type=jnp.float32)
        rounded = lax.optimization_barrier(partial_sum.astype(jnp.bfloat16))
        d_normed = d_normed + rounded.astype(jnp.float32)
    values_f = row_values.astype(jnp.float32)
    gain_part = lax.optimization_barrier(jnp.sum(d_normed * values_f * inverse, axis=0))
    scaled = d_normed * gain
    d_rows = cot_rows.astype(jnp.float32) + inverse * scaled - values_f * inverse * inverse * inverse * lax.optimization_barrier(jnp.mean(scaled * values_f, axis=1, keepdims=True))
    return (d_rows.astype(jnp.bfloat16), seq_terms, gain_part)

def reference(tokens, cotangent, gain, weights):
    seq_rows = TOK_DEV * N_CTX
    row_blocks = tokens.reshape(N_LOOP, seq_rows, D)
    cot_blocks = cotangent.reshape(N_LOOP, seq_rows, D)

    def advance(carry, item):
        grad_sum, gain_sum = carry
        d_rows, seq_terms, gain_part = sequence_grads(item[0], item[1], gain, weights)
        return ((grad_sum + seq_terms.astype(jnp.float32), gain_sum + gain_part), d_rows)
    start_carry = (jnp.zeros((D, 4, HEADS * HD), jnp.float32), jnp.zeros((D,), jnp.float32))
    (grad_sum, gain_sum), d_rows = lax.scan(advance, start_carry, (row_blocks, cot_blocks))
    loss_scale = 1.0 / math.sqrt(TOKENS)
    return (d_rows.reshape(TOKENS, D), grad_sum * loss_scale, gain_sum * loss_scale)
```

```python
import functools
import math

import jax
import jax.numpy as jnp
from jax import lax
from jax.experimental import pallas as pl
from jax.experimental.pallas import tpu as pltpu
from jax.sharding import PartitionSpec as P

HD = 128


EPS = 1e-05


def norm_rows(row_values, gain):
    values_f = row_values.astype(jnp.float32)
    inverse = lax.rsqrt(jnp.mean(values_f * values_f, axis=1, keepdims=True) + EPS)
    return (inverse, (values_f * inverse * gain).astype(jnp.bfloat16))


def rotate(values_f, offset, direction):
    amount = values_f.shape[0]
    half_width = values_f.shape[1] // 2
    position = (offset + jnp.arange(amount)).astype(jnp.float32)
    rates = jnp.exp(
        -math.log(10000.0) * jnp.arange(half_width).astype(jnp.float32) * 2.0 / values_f.shape[1]
    )
    angle = position[:, None] * rates[None, :]
    cosine = jnp.cos(angle)
    sine = jnp.sin(angle) * direction
    first_half = values_f[:, :half_width]
    second_half = values_f[:, half_width:]
    return jnp.concatenate(
        [first_half * cosine - second_half * sine, second_half * cosine + first_half * sine], axis=1
    )


def head_work(packed):
    query_head, key_head, value_head, grad_head = packed
    seq_rows = query_head.shape[0]
    width = query_head.shape[1]
    block_rows = min(512, seq_rows)
    scale = 1.0 / math.sqrt(width)
    rot_keys = rotate(key_head.astype(jnp.float32), 0, 1.0).astype(jnp.bfloat16)
    col_place = jnp.arange(seq_rows)

    def one_block(number):
        first_row = number * block_rows
        query_part = lax.dynamic_slice_in_dim(query_head, first_row, block_rows, 0).astype(
            jnp.float32
        )
        grad_part = lax.dynamic_slice_in_dim(grad_head, first_row, block_rows, 0)
        rot_query = rotate(query_part, first_row, 1.0).astype(jnp.bfloat16)
        scores = (
            lax.dot_general(
                rot_query, rot_keys, (((1,), (1,)), ((), ())), preferred_element_type=jnp.float32
            )
            * scale
        )
        row_place = first_row + jnp.arange(block_rows)
        scores = jnp.where(col_place[None, :] <= row_place[:, None], scores, -1e30)
        maximum = jnp.max(scores, axis=1, keepdims=True)
        expo = jnp.exp(scores - maximum)
        probs = expo / jnp.sum(expo, axis=1, keepdims=True)
        probs_low = probs.astype(jnp.bfloat16)
        output = jnp.dot(probs_low, value_head, preferred_element_type=jnp.float32)
        d_probs = lax.dot_general(
            grad_part, value_head, (((1,), (1,)), ((), ())), preferred_element_type=jnp.float32
        )
        delta = jnp.sum(grad_part.astype(jnp.float32) * output, axis=1, keepdims=True)
        d_scores = (probs * (d_probs - delta) * scale).astype(jnp.bfloat16)
        grad_query = rotate(
            jnp.dot(d_scores, rot_keys, preferred_element_type=jnp.float32), first_row, -1.0
        )
        rot_key_grad = lax.dot_general(
            d_scores, rot_query, (((0,), (0,)), ((), ())), preferred_element_type=jnp.float32
        )
        grad_values = lax.dot_general(
            probs_low, grad_part, (((0,), (0,)), ((), ())), preferred_element_type=jnp.float32
        )
        return (output, grad_query, rot_key_grad, grad_values)

    outputs, grad_query, rot_key_grad, grad_values = lax.map(
        one_block, jnp.arange(seq_rows // block_rows)
    )
    grad_keys = rotate(jnp.sum(rot_key_grad, axis=0), 0, -1.0)
    return (
        outputs.reshape(seq_rows, width),
        grad_query.reshape(seq_rows, width),
        grad_keys,
        jnp.sum(grad_values, axis=0),
    )


def contract_cols(left, right):
    return lax.dot_general(
        left, right, (((1,), (1,)), ((), ())), preferred_element_type=jnp.float32
    )


def plain_body(tokens, cotangent, gain, weights):
    loop_count = lax.axis_size("loop")
    inverse, normed = norm_rows(tokens, gain)
    full_normed, full_cot = (
        lax.all_gather(normed, "ctx", axis=0, tiled=True),
        lax.all_gather(cotangent, "ctx", axis=0, tiled=True),
    )
    seq_rows = full_normed.shape[0]
    width = weights.shape[2]
    whole = lax.all_gather(weights, "loop", axis=0, tiled=True)
    projected = jnp.stack(
        [
            jnp.dot(full_normed, whole[:, 0, :], preferred_element_type=jnp.float32),
            jnp.dot(full_normed, whole[:, 1, :], preferred_element_type=jnp.float32),
            jnp.dot(full_normed, whole[:, 2, :], preferred_element_type=jnp.float32),
            jnp.dot(full_cot, whole[:, 3, :], preferred_element_type=jnp.float32),
        ]
    )
    head_count = width // HD

    def split_heads(matrix):
        return matrix.astype(jnp.bfloat16).reshape(seq_rows, head_count, HD).transpose(1, 0, 2)

    def merge_heads(matrix):
        return matrix.transpose(1, 0, 2).reshape(seq_rows, width).astype(jnp.bfloat16)

    attn, grad_query, grad_keys, grad_values = lax.map(
        head_work,
        (
            split_heads(projected[0]),
            split_heads(projected[1]),
            split_heads(projected[2]),
            split_heads(projected[3]),
        ),
    )
    attn = merge_heads(attn)
    grad_query = merge_heads(grad_query)
    grad_keys = merge_heads(grad_keys)
    grad_values = merge_heads(grad_values)
    loss_scale = 1.0 / math.sqrt(seq_rows * loop_count)
    weight_grads = (
        lax.psum_scatter(
            jnp.stack(
                [
                    jnp.einsum(
                        "sd,sc->dc", full_normed, grad_query, preferred_element_type=jnp.float32
                    ),
                    jnp.einsum(
                        "sd,sc->dc", full_normed, grad_keys, preferred_element_type=jnp.float32
                    ),
                    jnp.einsum(
                        "sd,sc->dc", full_normed, grad_values, preferred_element_type=jnp.float32
                    ),
                    jnp.einsum("sd,sc->dc", full_cot, attn, preferred_element_type=jnp.float32),
                ],
                axis=1,
            ).astype(jnp.bfloat16),
            "loop",
            scatter_dimension=0,
            tiled=True,
        ).astype(jnp.float32)
        * loss_scale
    )
    partial_sum = (
        contract_cols(grad_query, whole[:, 0, :])
        + contract_cols(grad_keys, whole[:, 1, :])
        + contract_cols(grad_values, whole[:, 2, :])
    ).astype(jnp.bfloat16)
    d_normed = lax.psum_scatter(partial_sum, "ctx", scatter_dimension=0, tiled=True).astype(
        jnp.float32
    )
    values_f = tokens.astype(jnp.float32)
    gain_part = jnp.sum(d_normed * values_f * inverse, axis=0)
    gain_grad = lax.psum(gain_part, ("loop", "ctx")) * loss_scale
    scaled = d_normed * gain
    d_rows = (
        cotangent.astype(jnp.float32)
        + inverse * scaled
        - values_f
        * inverse
        * inverse
        * inverse
        * jnp.mean(scaled * values_f, axis=1, keepdims=True)
    )
    return (d_rows.astype(jnp.bfloat16), weight_grads, gain_grad)


F32 = jnp.float32
BF16 = jnp.bfloat16
VMEM_LIMIT = 56 * 1024 * 1024


def bits_of(count):
    return count.bit_length() - 1


def is_power(count):
    return count >= 1 and count & (count - 1) == 0


def reverse_bits(number, width):
    return sum(((number >> i) & 1) << (width - 1 - i) for i in range(width))


def full_spec(shape):
    return pl.BlockSpec(shape, lambda *_: (0,) * len(shape))


def params():
    return pltpu.CompilerParams(vmem_limit_bytes=VMEM_LIMIT)


def prepare(order, tokens, cotangent, gain_row):
    rows, features = tokens.shape
    blocks = order.shape[0]
    wide = features // blocks

    def kernel(order_ref, tok_ref, cot_ref, gain_ref, normed_ref, cot_out_ref):
        values_f = tok_ref[...].astype(F32)
        inverse = lax.rsqrt(jnp.mean(values_f * values_f, axis=1, keepdims=True) + EPS)
        for place in range(blocks):
            cols = pl.ds(pl.multiple_of(order_ref[place] * wide, wide), wide)
            out = slice(place * wide, (place + 1) * wide)
            normed_ref[:, out] = (tok_ref[:, cols].astype(F32) * inverse * gain_ref[:, cols]).astype(BF16)
            cot_out_ref[:, out] = cot_ref[:, cols]

    return pl.pallas_call(
        kernel,
        out_shape=[jax.ShapeDtypeStruct(tokens.shape, BF16)] * 2,
        grid=(1,),
        in_specs=[pl.BlockSpec(memory_space=pltpu.SMEM)]
        + [full_spec(tokens.shape)] * 2
        + [full_spec(gain_row.shape)],
        out_specs=[full_spec(tokens.shape)] * 2,
        compiler_params=params(),
        name="prepare",
    )(order, tokens, cotangent, gain_row)


def swapped_columns(places, chip_bits):
    result = []
    for place in range(places):
        result.append((reverse_bits(place >> 1, chip_bits) << 1) | ((place & 1) ^ 1))
    return result


def rows_product(own, partner, stacked, first_block, col_blocks, wide, chip_bits):
    rows, features = own[0].shape
    places = 2 << chip_bits
    step = features // places
    swap = swapped_columns(places, chip_bits)
    count = len(own) + len(partner)
    total = count * rows

    def kernel(*refs):
        inputs, w_ref, out_ref, held = refs[:count], refs[count], refs[count + 1], refs[count + 2]

        @pl.when(pl.program_id(0) == 0)
        def _():
            for number, ref in enumerate(inputs):
                here = slice(number * rows, (number + 1) * rows)
                if number < len(own):
                    held[here, :] = ref[...]
                else:
                    for place in range(places):
                        source = swap[place]
                        held[here, place * step : (place + 1) * step] = ref[
                            :, source * step : (source + 1) * step
                        ]

        out_ref[...] = jnp.dot(held[...], w_ref[...], preferred_element_type=F32).astype(BF16)

    return pl.pallas_call(
        kernel,
        out_shape=jax.ShapeDtypeStruct((total, col_blocks * wide), BF16),
        grid=(col_blocks,),
        in_specs=[full_spec((rows, features))] * count
        + [pl.BlockSpec((features, wide), lambda i: (0, first_block + i))],
        out_specs=pl.BlockSpec((total, wide), lambda i: (0, i)),
        scratch_shapes=[pltpu.VMEM((total, features), BF16)],
        compiler_params=params(),
        name="rows_product",
    )(*own, *partner, stacked)


def turn(values_f, cosine, sine, direction):
    return values_f * cosine + direction * pltpu.roll(values_f, HD // 2, 1) * sine


def attention_forward(projected, first_row, seq_rows, heads, cosine, sine, row_place, col_place):
    scale = 1.0 / math.sqrt(HD)

    def kernel(q_ref, k_ref, v_ref, cos_ref, sin_ref, row_ref, col_ref, attn_ref, probs_ref):
        cos, sin = cos_ref[...], sin_ref[...]
        rot_query = turn(q_ref[...].astype(F32), cos, sin, 1.0).astype(BF16)
        rot_keys = turn(k_ref[...].astype(F32), cos, sin, 1.0).astype(BF16)
        scores = lax.dot_general(
            rot_query, rot_keys, (((1,), (1,)), ((), ())), preferred_element_type=F32
        ) * scale
        scores = jnp.where(col_ref[...] <= row_ref[...], scores, -1e30)
        expo = jnp.exp(scores - jnp.max(scores, axis=1, keepdims=True))
        probs = (expo / jnp.sum(expo, axis=1, keepdims=True)).astype(BF16)
        probs_ref[0] = probs
        attn_ref[...] = jnp.dot(probs, v_ref[...], preferred_element_type=F32).astype(BF16)

    block = first_row // seq_rows
    return pl.pallas_call(
        kernel,
        out_shape=[
            jax.ShapeDtypeStruct((seq_rows, heads * HD), BF16),
            jax.ShapeDtypeStruct((heads, seq_rows, seq_rows), BF16),
        ],
        grid=(heads,),
        in_specs=[
            pl.BlockSpec((seq_rows, HD), lambda h: (block, h)),
            pl.BlockSpec((seq_rows, HD), lambda h: (block, heads + h)),
            pl.BlockSpec((seq_rows, HD), lambda h: (block, 2 * heads + h)),
            full_spec((seq_rows, HD)),
            full_spec((seq_rows, HD)),
            full_spec((seq_rows, 1)),
            full_spec((1, seq_rows)),
        ],
        out_specs=[
            pl.BlockSpec((seq_rows, HD), lambda h: (0, h)),
            pl.BlockSpec((1, seq_rows, seq_rows), lambda h: (h, 0, 0)),
        ],
        compiler_params=params(),
        name="attention_forward",
    )(projected, projected, projected, cosine, sine, row_place, col_place)


def attention_backward(projected, first_row, seq_rows, heads, d_attn, probs, cosine, sine):
    scale = 1.0 / math.sqrt(HD)
    width = heads * HD

    def kernel(q_ref, k_ref, v_ref, d_ref, probs_ref, cos_ref, sin_ref, out_ref):
        cos, sin = cos_ref[...], sin_ref[...]
        rot_query = turn(q_ref[...].astype(F32), cos, sin, 1.0).astype(BF16)
        rot_keys = turn(k_ref[...].astype(F32), cos, sin, 1.0).astype(BF16)
        grad_rows, probs_low = d_ref[...], probs_ref[0]
        d_probs = lax.dot_general(
            grad_rows, v_ref[...], (((1,), (1,)), ((), ())), preferred_element_type=F32
        )
        probs_f = probs_low.astype(F32)
        delta = jnp.sum(probs_f * d_probs, axis=1, keepdims=True)
        d_scores = (probs_f * (d_probs - delta) * scale).astype(BF16)
        grad_query = jnp.dot(d_scores, rot_keys, preferred_element_type=F32)
        grad_keys = lax.dot_general(
            d_scores, rot_query, (((0,), (0,)), ((), ())), preferred_element_type=F32
        )
        grad_values = lax.dot_general(
            probs_low, grad_rows, (((0,), (0,)), ((), ())), preferred_element_type=F32
        )
        first = pl.multiple_of(pl.program_id(0) * HD, HD)
        out_ref[:, pl.ds(first, HD)] = turn(grad_query, cos, sin, -1.0).astype(BF16)
        out_ref[:, pl.ds(width + first, HD)] = turn(grad_keys, cos, sin, -1.0).astype(BF16)
        out_ref[:, pl.ds(2 * width + first, HD)] = grad_values.astype(BF16)

    block = first_row // seq_rows
    return pl.pallas_call(
        kernel,
        out_shape=jax.ShapeDtypeStruct((seq_rows, 3 * width), BF16),
        grid=(heads,),
        in_specs=[
            pl.BlockSpec((seq_rows, HD), lambda h: (block, h)),
            pl.BlockSpec((seq_rows, HD), lambda h: (block, heads + h)),
            pl.BlockSpec((seq_rows, HD), lambda h: (block, 2 * heads + h)),
            pl.BlockSpec((seq_rows, HD), lambda h: (0, h)),
            pl.BlockSpec((1, seq_rows, seq_rows), lambda h: (h, 0, 0)),
            full_spec((seq_rows, HD)),
            full_spec((seq_rows, HD)),
        ],
        out_specs=full_spec((seq_rows, 3 * width)),
        compiler_params=params(),
        name="attention_backward",
    )(projected, projected, projected, d_attn, probs, cosine, sine)


def weight_term(own, partner, left, right, member, wide, chip, chip_bits):
    rows, features = own[0].shape
    tall = features >> chip_bits
    half = tall // 2
    count = len(own)
    other = reverse_bits(chip, chip_bits)
    seq_rows = rows * count

    def kernel(*refs):
        left_ref, right_ref, out_ref, held = refs[2 * count :]
        for number in range(count):
            held[number * rows : (number + 1) * rows, :] = refs[number][...]
            source = refs[count + number]
            here = slice(seq_rows + number * rows, seq_rows + (number + 1) * rows)
            held[here, :half] = source[:, half:]
            held[here, half:] = source[:, :half]
        contract = (((0,), (0,)), ((), ()))
        total = lax.dot_general(
            held[:seq_rows], left_ref[...], contract, preferred_element_type=F32
        ) + lax.dot_general(held[seq_rows:], right_ref[...], contract, preferred_element_type=F32)
        out_ref[...] = total.astype(BF16)

    return pl.pallas_call(
        kernel,
        out_shape=jax.ShapeDtypeStruct((tall, wide), BF16),
        grid=(1,),
        in_specs=[pl.BlockSpec((rows, tall), lambda i: (0, chip))] * count
        + [pl.BlockSpec((rows, tall), lambda i: (0, other))] * count
        + [pl.BlockSpec((seq_rows, wide), lambda i: (0, member))] * 2,
        out_specs=full_spec((tall, wide)),
        scratch_shapes=[pltpu.VMEM((2 * seq_rows, tall), BF16)],
        compiler_params=params(),
        name="weight_term",
    )(*own, *partner, left, right)


def input_grad(grads, stacked, chip_bits, for_partner, received=None):
    seq_rows, depth = grads.shape
    features = stacked.shape[0]
    chips = 1 << chip_bits
    tall = features >> chip_bits
    half = tall // 2

    def kernel(*refs):
        grad_ref, w_ref, out_ref = refs[0], refs[1], refs[-1]
        part = lax.dot_general(
            grad_ref[...], w_ref[...], (((1,), (1,)), ((), ())), preferred_element_type=F32
        )
        if for_partner:
            out_ref[:, half:] = part[:, :half].astype(BF16)
            out_ref[:, :half] = part[:, half:].astype(BF16)
        else:
            out_ref[...] = (part + refs[2][...].astype(F32)).astype(BF16)

    place = [reverse_bits(chip, chip_bits) for chip in range(chips)]

    def out_map(chip):
        if not for_partner:
            return (0, chip)
        where = chip * 0
        for number in range(chips):
            where = where + jnp.where(chip == number, place[number], 0)
        return (0, where)

    extra = [] if for_partner else [received]
    return pl.pallas_call(
        kernel,
        out_shape=jax.ShapeDtypeStruct((seq_rows, features), BF16),
        grid=(chips,),
        in_specs=[
            full_spec((seq_rows, depth)),
            pl.BlockSpec((tall, depth), lambda chip: (chip, 0)),
        ]
        + [pl.BlockSpec((seq_rows, tall), lambda chip: (0, chip))] * len(extra),
        out_specs=pl.BlockSpec((seq_rows, tall), out_map),
        compiler_params=params(),
        name="input_grad",
    )(grads, stacked, *extra)


def gain_term(order, d_rows, own):
    seq_rows, features = d_rows.shape
    rows = own[0].shape[0]
    blocks = order.shape[0]
    wide = features // blocks

    def kernel(order_ref, d_ref, *refs):
        total = jnp.zeros((1, wide), F32)
        for number in range(len(own)):
            here = slice(number * rows, (number + 1) * rows)
            total = total + jnp.sum(
                d_ref[here, :].astype(F32) * refs[number][...].astype(F32), axis=0, keepdims=True
            )
        refs[-1][...] = total

    return pl.pallas_call(
        kernel,
        out_shape=jax.ShapeDtypeStruct((1, features), F32),
        grid_spec=pltpu.PrefetchScalarGridSpec(
            num_scalar_prefetch=1,
            grid=(blocks,),
            in_specs=[pl.BlockSpec((seq_rows, wide), lambda t, order: (0, t))]
            + [pl.BlockSpec((rows, wide), lambda t, order: (0, t))] * len(own),
            out_specs=pl.BlockSpec((1, wide), lambda t, order: (0, order[t])),
        ),
        compiler_params=params(),
        name="gain_term",
    )(order, d_rows, *own)


def finish_tokens(order, parts, tokens, cotangent, gain_row):
    rows, features = tokens.shape
    blocks = order.shape[0]
    wide = features // blocks

    def kernel(order_ref, tok_ref, cot_ref, gain_ref, *refs):
        out_ref = refs[-1]
        values_f = tok_ref[...].astype(F32)
        inverse = lax.rsqrt(jnp.mean(values_f * values_f, axis=1, keepdims=True) + EPS)
        dot = jnp.zeros((rows, 1), F32)
        for place in range(blocks):
            cols = pl.ds(pl.multiple_of(order_ref[place] * wide, wide), wide)
            here = slice(place * wide, (place + 1) * wide)
            d_part = sum(ref[:, here].astype(F32) for ref in refs[:-1])
            scaled = d_part * gain_ref[:, cols]
            dot = dot + jnp.sum(scaled * tok_ref[:, cols].astype(F32), axis=1, keepdims=True)
        shift = inverse * inverse * inverse * (dot / features)
        for place in range(blocks):
            cols = pl.ds(pl.multiple_of(order_ref[place] * wide, wide), wide)
            here = slice(place * wide, (place + 1) * wide)
            d_part = sum(ref[:, here].astype(F32) for ref in refs[:-1])
            out_ref[:, cols] = (
                cot_ref[:, cols].astype(F32)
                + inverse * (d_part * gain_ref[:, cols])
                - tok_ref[:, cols].astype(F32) * shift
            ).astype(BF16)

    return pl.pallas_call(
        kernel,
        out_shape=jax.ShapeDtypeStruct(tokens.shape, BF16),
        grid=(1,),
        in_specs=[pl.BlockSpec(memory_space=pltpu.SMEM)]
        + [full_spec(tokens.shape)] * 2
        + [full_spec(gain_row.shape)]
        + [full_spec(tokens.shape)] * len(parts),
        out_specs=full_spec(tokens.shape),
        compiler_params=params(),
        name="finish_tokens",
    )(order, tokens, cotangent, gain_row, *parts)


def spread(block, steps):
    blocks = [block]
    for step in steps:
        blocks = blocks + [step(one) for one in blocks]
    return blocks


def paired_body(loop_count, ctx_count, tokens, cotangent, gain, weights):
    chip_bits = bits_of(loop_count) - 1
    ctx_bits = bits_of(ctx_count)
    places = loop_count
    rows, features = tokens.shape
    width = weights.shape[2]
    half = width // 2
    heads = half // HD
    seq_rows = rows * ctx_count
    me = lax.axis_index("loop")
    here = lax.axis_index("ctx")
    core = me % 2

    def chip_mask(number, which):
        return 1 << (number if which == 0 else chip_bits - 1 - number)

    def ctx_mask(number, which):
        return 1 << (ctx_bits - 1 - number if which == 0 else number)

    def loop_step(number):
        pairs = [(l, l ^ (chip_mask(number, l % 2) << 1)) for l in range(loop_count)]
        return lambda array: lax.ppermute(array, "loop", pairs)

    def ctx_step(number):
        pairs = []
        for l in range(loop_count):
            for c in range(ctx_count):
                pairs.append((l * ctx_count + c, l * ctx_count + (c ^ ctx_mask(number, l % 2))))
        return lambda array: lax.ppermute(array, ("loop", "ctx"), pairs)

    def to_partner(array):
        return lax.ppermute(array, "loop", [(l, l ^ 1) for l in range(loop_count)])

    loop_steps = [loop_step(number) for number in range(chip_bits)]
    ctx_steps = [ctx_step(number) for number in range(ctx_bits)]

    def mask_of(index, bits, mask, which):
        return sum(mask(number, which) for number in range(bits) if (index >> number) & 1)

    order = []
    for place in range(places):
        masks = [mask_of(place >> 1, chip_bits, chip_mask, which) << 1 for which in (0, 1)]
        order.append(me ^ (place & 1) ^ jnp.where(core == 0, masks[0], masks[1]))
    order = jnp.stack(order).astype(jnp.int32)

    def places_of(which_core):
        chunks = []
        for index in range(ctx_count):
            masks = [mask_of(index, ctx_bits, ctx_mask, which) for which in (0, 1)]
            chunk = here ^ jnp.where(which_core == 0, masks[0], masks[1])
            chunks.append(chunk * rows + jnp.arange(rows))
        return jnp.concatenate(chunks)

    def tables(place):
        rates = jnp.exp(
            -math.log(10000.0) * jnp.arange(HD // 2).astype(F32) * 2.0 / HD
        )
        angle = place.astype(F32)[:, None] * rates[None, :]
        cosine, sine = jnp.cos(angle), jnp.sin(angle)
        return (
            jnp.concatenate([cosine, cosine], axis=1),
            jnp.concatenate([-sine, sine], axis=1),
            place[:, None],
            place[None, :],
        )

    gain_row = gain.reshape(1, features)
    normed, cot = prepare(order, tokens, cotangent, gain_row)
    own_n = spread(normed, ctx_steps)
    own_c = spread(cot, ctx_steps)
    partner_n = [to_partner(one) for one in own_n]
    partner_c = [to_partner(one) for one in own_c]

    halves = weights.reshape(weights.shape[0], weights.shape[1], 2, half)
    mine = lax.dynamic_index_in_dim(halves, core, 2, keepdims=False)
    theirs = lax.dynamic_index_in_dim(halves, 1 - core, 2, keepdims=False)
    flat = (weights.shape[0], weights.shape[1] * half)
    first = spread(mine.reshape(flat), loop_steps)
    second = spread(to_partner(theirs.reshape(flat)), loop_steps)
    stacked = jnp.concatenate([one for pair in zip(first, second) for one in pair], axis=0)

    own_tables = tables(places_of(core))
    partner_tables = tables(places_of(1 - core))

    projected = rows_product(own_n, partner_n, stacked, 0, 3, half, chip_bits)
    attn_own, probs_own = attention_forward(projected, 0, seq_rows, heads, *own_tables)
    attn_partner, probs_partner = attention_forward(
        projected, seq_rows, seq_rows, heads, *partner_tables
    )
    last = ctx_count - 1
    early = rows_product(own_c[:last], partner_c[:last], stacked, 3, 1, half, chip_bits)
    late = rows_product(own_c[last:], partner_c[last:], stacked, 3, 1, half, chip_bits)
    d_own = jnp.concatenate([early[: rows * last], late[:rows]], axis=0)
    d_partner = jnp.concatenate([early[rows * last :], late[rows:]], axis=0)

    loss_scale = 1.0 / math.sqrt(seq_rows * loop_count)

    def reduced(left_rows, right_rows, left, right, member):
        chips = 1 << chip_bits
        blocks = [None] * chips
        for chip in reversed(range(chips)):
            blocks[chip] = weight_term(
                left_rows, right_rows, left, right, member, half, chip, chip_bits
            )
        return blocks

    def gathered(blocks, steps):
        sums = [[one] for one in blocks]
        for step in reversed(steps):
            middle = len(sums) // 2
            sent = []
            for group in sums[middle:]:
                if len(group) == 1:
                    sent.append(step(group[0]))
                else:
                    sent.append(step(sum(one.astype(F32) for one in group).astype(BF16)))
            sums = [group + [one] for group, one in zip(sums[:middle], sent)]
        return sums[0]

    def settled(blocks):
        total = sum(one.astype(F32) for one in gathered(blocks, loop_steps))
        tall = total.shape[0] // 2
        return (total[:tall], to_partner(total[tall:].astype(BF16)).astype(F32))

    out_blocks = reduced(own_c, partner_c, attn_own, attn_partner, 0)
    out_done = settled(out_blocks)

    grads_own = attention_backward(
        projected, 0, seq_rows, heads, d_own, probs_own, own_tables[0], own_tables[1]
    )
    grads_partner = attention_backward(
        projected, seq_rows, seq_rows, heads, d_partner, probs_partner,
        partner_tables[0], partner_tables[1],
    )
    d_sent = to_partner(input_grad(grads_partner, stacked, chip_bits, True))
    d_sum = input_grad(grads_own, stacked, chip_bits, False, d_sent)
    d_parts = gathered([d_sum[rows * i : rows * (i + 1)] for i in range(ctx_count)], ctx_steps)
    gain_part = gain_term(order, d_sum, own_n)
    for number in range(bits_of(loop_count)):
        pairs = [(l, l ^ (1 << number)) for l in range(loop_count)]
        gain_part = gain_part + lax.ppermute(gain_part, "loop", pairs)
    for number in range(ctx_bits):
        pairs = [(c, c ^ (1 << number)) for c in range(ctx_count)]
        gain_part = gain_part + lax.ppermute(gain_part, "ctx", pairs)
    gain_grad = gain_part.reshape(features) * loss_scale / gain

    done = [
        settled(reduced(own_n, partner_n, grads_own, grads_partner, member)) for member in range(3)
    ]
    done.append(out_done)
    ours = jnp.stack([one[0] for one in done], axis=1) * loss_scale
    others = jnp.stack([one[1] for one in done], axis=1) * loss_scale
    weight_grads = jnp.where(
        core == 0,
        jnp.concatenate([ours, others], axis=2),
        jnp.concatenate([others, ours], axis=2),
    )
    d_tokens = finish_tokens(order, d_parts, tokens, cotangent, gain_row)
    return (d_tokens, weight_grads, gain_grad)


def body(loop_count, ctx_count, tokens, cotangent, gain, weights):
    width = weights.shape[2]
    paired = (
        is_power(loop_count)
        and is_power(ctx_count)
        and loop_count > 1
        and ctx_count > 1
        and width % (2 * HD) == 0
        and weights.shape[0] % HD == 0
    )
    if paired:
        return paired_body(loop_count, ctx_count, tokens, cotangent, gain, weights)
    return plain_body(tokens, cotangent, gain, weights)


def solution(mesh):

    return jax.shard_map(
        functools.partial(body, mesh.shape["loop"], mesh.shape["ctx"]),
        mesh=mesh,
        in_specs=(P(("loop", "ctx"), None), P(("loop", "ctx"), None), P(), P("loop", None, "ctx")),
        out_specs=(P(("loop", "ctx"), None), P("loop", None, "ctx"), P()),
        check_vma=False,
    )
```
